128 devices in a mesh: row: 8 (over z, core), col: 16 (over x, y).
Axes of the slice: x: 4, y: 4, z: 4, core: 2. Of those that a mesh axis runs over, the one named last changes fastest.
Arguments:
- tile_data: bfloat16 [8, 16, 256, 128, 128], P('row', 'col')
- tile_rows: int32 [8, 16, 256], P('row', 'col'), may hold values from 0 to 15, as said below
- tile_cols: int32 [8, 16, 256], P('row', 'col'), may hold values from 0 to 31
- tile_count: int32 [8, 16], P('row', 'col'), may hold values from 32 to 256, as said below
- sketch: bfloat16 [65536, 256], P('col')
Outputs:
- range_one: float32 [16384, 256], P(('row', 'col'))
- basis: float32 [16384, 256], P(('row', 'col'))
The draws below stay inside these ranges and needn't reach their ends.
Inputs may be any that keep to these rules, and one draw needn't show every extreme that they name: On each device the pairs (tile_rows, tile_cols) are distinct. A device's live tiles are its first tile_count tiles; the rest are padding.
All inputs are finite; a program needn't handle non-finite values.
Results may differ from the reference program's by a relative error of at most 0.0028.
Values may be sent and summed in bfloat16 or wider, within the bound.
A program may use at most 128 MiB of HBM per device.

```python
import math
import jax
import jax.numpy as jnp
from jax import lax

TILE = 128
K = 256
RB_G = 16
CB_G = 32
TILES_DEV = 256
ROWS = 16384
COLS = 65536
N_ROW = 8
N_COL = 16


def tile_positions(key):
    base = jax.random.fold_in(key, 11)
    keys = jax.random.split(base, N_ROW * N_COL)
    perms = jax.vmap(lambda k: jax.random.permutation(k, RB_G * CB_G))(keys)[:, :TILES_DEV]
    return perms.reshape(N_ROW, N_COL, TILES_DEV).astype(jnp.int32)


def draw_tile_rows(key, part):
    return (tile_positions(key) // CB_G).astype(jnp.int32)


def draw_tile_cols(key, part):
    return (tile_positions(key) % CB_G).astype(jnp.int32)


def draw_tile_count(key, part):
    total = N_ROW * N_COL
    shifts = jax.random.randint(jax.random.fold_in(key, 21), (total,), 0, 4)
    counts = jnp.floor_divide(TILES_DEV, jnp.left_shift(1, shifts)).astype(jnp.int32)
    top = jax.random.randint(jax.random.fold_in(key, 22), (), 0, total)
    other = (top + 1 + jax.random.randint(jax.random.fold_in(key, 23), (), 0, total - 1)) % total
    counts = counts.at[top].set(TILES_DEV).at[other].set(TILES_DEV // 8)
    return counts.reshape(N_ROW, N_COL).astype(jnp.int32)


def draw_tile_data(key, part):
    shape = (N_ROW, N_COL, TILES_DEV, TILE, TILE)
    first_key = jax.random.fold_in(key, 31)
    second_key = jax.random.fold_in(key, 32)
    values = jax.random.normal(first_key, shape, jnp.float32)
    groups = 1.0 + 2.0 * jnp.arange(N_ROW, dtype=jnp.float32) / max(N_ROW - 1, 1)
    spread = jnp.exp(jax.random.uniform(second_key, (N_ROW, N_COL, TILES_DEV, 1, 1), jnp.float32, -0.7, 0.7))
    fan = TILES_DEV * TILE * N_COL / RB_G
    return (values * groups[:, None, None, None, None] * spread / math.sqrt(fan)).astype(jnp.bfloat16)


def draw_sketch(key, part):
    noise_key = jax.random.fold_in(key, 41)
    common_key = jax.random.fold_in(key, 42)
    weight_key = jax.random.fold_in(key, 43)
    values = jax.random.normal(noise_key, (COLS, K), jnp.float32)
    common = jax.random.normal(common_key, (COLS, 1), jnp.float32)
    column_load = jnp.exp(jax.random.uniform(weight_key, (1, K), jnp.float32, -0.7, 0.0))
    return (values + column_load * common).astype(jnp.bfloat16)


def setup_inputs(seed: int = 0) -> dict:
    streams_of = jax.random.split(jax.random.key(seed), 6)
    return {
        "tile_data": draw_tile_data(jax.random.fold_in(streams_of[5], 71), 0),
        "tile_rows": draw_tile_rows(jax.random.fold_in(streams_of[5], 71), 0),
        "tile_cols": draw_tile_cols(jax.random.fold_in(streams_of[5], 71), 0),
        "tile_count": draw_tile_count(jax.random.fold_in(streams_of[5], 71), 0),
        "sketch": draw_sketch(jax.random.fold_in(streams_of[5], 71), 0),
    }


def apply_tiles(tile_data, out_index, in_index, live, operand, n_out, flip):
    devices = N_ROW * N_COL
    form = 'tba,tbk->tak' if flip else 'tab,tbk->tak'

    def one_device(total, items):
        tiles, target, source, weight = items
        rows = operand[source].astype(jnp.float32)
        product = jnp.einsum(form, tiles.astype(jnp.float32), rows, precision=lax.Precision.HIGHEST)
        product = product * weight[:, None, None]
        return (total.at[target].add(product), None)
    start = jnp.zeros((n_out, TILE, K), jnp.float32)
    items = (tile_data.reshape(devices, TILES_DEV, TILE, TILE), out_index.reshape(devices, TILES_DEV), in_index.reshape(devices, TILES_DEV), live.reshape(devices, TILES_DEV))
    total, unused = lax.scan(one_device, start, items)
    return total

def orthonormal(values):
    gram = jnp.dot(values.T, values, precision=lax.Precision.HIGHEST)
    lower = jnp.linalg.cholesky(gram)
    inverse = lax.linalg.triangular_solve(lower, jnp.eye(K, dtype=jnp.float32), left_side=True, lower=True)
    return jnp.dot(values, inverse.T, precision=lax.Precision.HIGHEST)

def reference(tile_data, tile_rows, tile_cols, tile_count, sketch):
    global_rows = (tile_rows + (jnp.arange(N_ROW, dtype=jnp.int32) * RB_G)[:, None, None]).astype(jnp.int32)
    global_cols = (tile_cols + (jnp.arange(N_COL, dtype=jnp.int32) * CB_G)[None, :, None]).astype(jnp.int32)
    live = (jnp.arange(TILES_DEV, dtype=jnp.int32)[None, None, :] < tile_count[:, :, None]).astype(jnp.float32)
    omega = sketch.reshape(N_COL * CB_G, TILE, K)
    first = apply_tiles(tile_data, global_rows, global_cols, live, omega, N_ROW * RB_G, False).reshape(ROWS, K)
    ortho_float = orthonormal(first)
    range_one = ortho_float * math.sqrt(ROWS)
    ortho_one = ortho_float.astype(jnp.bfloat16)
    cross = apply_tiles(tile_data, global_cols, global_rows, live, ortho_one.reshape(N_ROW * RB_G, TILE, K), N_COL * CB_G, True)
    cross = cross.astype(jnp.bfloat16)
    second = apply_tiles(tile_data, global_rows, global_cols, live, cross, N_ROW * RB_G, False).reshape(ROWS, K)
    return (range_one, orthonormal(second) * math.sqrt(ROWS))
```

```python
import math

import jax
import jax.numpy as jnp
from jax import lax
from jax.experimental import pallas as pl
from jax.experimental.pallas import tpu as pltpu
from jax.sharding import PartitionSpec as P

MESH = pl.DeviceIdType.MESH
F32, BF16 = jnp.float32, jnp.bfloat16
HI = lax.Precision.HIGHEST
TILE, K, RB, CB = 128, 256, 16, 32
ROWS_DEV, COLS_DEV = RB * TILE, CB * TILE
COPIES = 176


def flip(c, e):
    if e == 1:
        return c + 1 - 2 * (c % 2)
    if e == 2:
        return (c + 2) % 4
    return 3 - c


ORDERS = ((0, 1, 3), (0, 3, 1), (1, 1, 3), (1, 3, 1))


class Net:
    def __init__(self, send, recv):
        self.send, self.recv, self.count = send, recv, 0
        self.open = []
        r, c = lax.axis_index("row"), lax.axis_index("col")
        self.z, self.core, self.x, self.y = r // 2, r % 2, c // 4, c % 4
        self.row, self.col = r, c

    def to(self, x=None, y=None, z=None, core=None):
        x = self.x if x is None else x
        y = self.y if y is None else y
        z = self.z if z is None else z
        core = self.core if core is None else core
        return (z * 2 + core, x * 4 + y)

    def start(self, src, dst, device):
        n = self.count
        self.count += 1
        copy = pltpu.make_async_remote_copy(
            src_ref=src, dst_ref=dst, send_sem=self.send.at[n], recv_sem=self.recv.at[n],
            device_id=device, device_id_type=MESH,
        )
        copy.start()
        self.open.append(copy)
        return copy

    def close(self):
        for copy in self.open:
            copy.wait_send()
        self.open = []


def at2(ref, axis, a, b, *rest):
    return ref.at[(a, b, *rest)] if axis == 0 else ref.at[(b, a, *rest)]


ALL = slice(None)


def reduce_scatter(net, part, r0, r1, r2, r3):
    pos = (net.x, net.y)

    def peer(axis, e):
        return net.to(x=flip(net.x, e)) if axis == 0 else net.to(y=flip(net.y, e))

    def add(axis, a, b, q, value):
        ref = at2(part, axis, a, b, q)
        ref[...] = ref[...] + value

    copies = []
    for q, (axis, e, g) in enumerate(ORDERS):
        c = pos[axis]
        copies.append([
            net.start(at2(part, axis, flip(c, e), ALL, q), r0.at[q, 0], peer(axis, e)),
            net.start(at2(part, axis, flip(c, 2), ALL, q), r0.at[q, 1], peer(axis, e)),
        ])
    for q, (axis, e, g) in enumerate(ORDERS):
        c = pos[axis]
        copies[q][1].wait_recv()
        add(axis, flip(c, g), ALL, q, r0[q, 1])
        copies[q].append(net.start(at2(part, axis, flip(c, g), ALL, q), r1.at[q], peer(axis, g)))
        copies[q][0].wait_recv()
        add(axis, c, ALL, q, r0[q, 0])
    for q, (axis, e, g) in enumerate(ORDERS):
        c, d, other = pos[axis], pos[1 - axis], 1 - axis
        copies[q][2].wait_recv()
        add(axis, c, ALL, q, r1[q])
        copies[q].append(net.start(at2(part, other, flip(d, e), c, q), r2.at[q, 0], peer(other, e)))
        copies[q].append(net.start(at2(part, other, flip(d, 2), c, q), r2.at[q, 1], peer(other, e)))
    for q, (axis, e, g) in enumerate(ORDERS):
        c, d, other = pos[axis], pos[1 - axis], 1 - axis
        copies[q][4].wait_recv()
        add(axis, c, flip(d, g), q, r2[q, 1])
        copies[q].append(net.start(at2(part, other, flip(d, g), c, q), r3.at[q], peer(other, g)))
        copies[q][3].wait_recv()
        add(axis, c, d, q, r2[q, 0])
    for q, (axis, e, g) in enumerate(ORDERS):
        copies[q][5].wait_recv()
        add(axis, pos[axis], pos[1 - axis], q, r3[q])


class Gather:
    def __init__(self, net, buf):
        self.net, self.buf, self.step, self.flying = net, buf, 0, []

    def advance(self):
        net, buf, t = self.net, self.buf, self.step
        for copy in self.flying:
            copy.wait_recv()
        self.flying = []
        self.step += 1
        if t == 4:
            return
        pos = (net.x, net.y)
        for q, (axis, e, g) in enumerate(ORDERS):
            c, d, other = pos[axis], pos[1 - axis], 1 - axis
            link = (axis, e) if t == 0 else (axis, g) if t == 1 else (other, e) if t == 2 else (other, g)
            dev = net.to(x=flip(net.x, link[1])) if link[0] == 0 else net.to(y=flip(net.y, link[1]))
            if t == 0:
                parts = [(c, d)]
            elif t == 1:
                parts = [(c, d), (flip(c, e), d)]
            elif t == 2:
                parts = [(ALL, d)]
            else:
                parts = [(ALL, d), (ALL, flip(d, e))]
            for a, b in parts:
                ref = at2(buf, axis, a, b, q)
                self.flying.append(net.start(ref, ref, dev))


class GramSum:
    def __init__(self, net, g, h, r0, r1, r2, ga, out):
        self.net, self.g, self.h, self.r0, self.r1, self.r2, self.ga, self.out = net, g, h, r0, r1, r2, ga, out
        self.phase, self.flying = 0, []

    def advance(self):
        net, half = self.net, K // 2
        for copy in self.flying:
            copy.wait_recv()
        self.flying = []
        phase = self.phase
        self.phase += 1
        other = net.to(core=1 - net.core)
        mine = pl.ds(pl.multiple_of(net.core * half, half), half)
        theirs = pl.ds(pl.multiple_of((1 - net.core) * half, half), half)
        if phase == 0:
            self.flying.append(net.start(self.g.at[theirs], self.r0, other))
        elif phase == 1:
            self.h[...] = (self.g[mine, :] + self.r0[...]).reshape(16, 8, K)
            for n in range(1, 16):
                j = (net.col + n) % 16
                self.flying.append(net.start(self.h.at[j], self.r1.at[n], (net.row, j)))
            self.r1[0] = self.h[net.col]
        elif phase == 2:
            self.r2[net.z] = jnp.sum(self.r1[...], axis=0)
            for n in range(1, 4):
                z = (net.z + n) % 4
                self.flying.append(net.start(self.r2.at[net.z], self.r2.at[net.z], net.to(z=z)))
        elif phase == 3:
            self.ga[net.col] = jnp.sum(self.r2[...], axis=0)
            for n in range(1, 16):
                j = (net.col + n) % 16
                self.flying.append(net.start(self.ga.at[net.col], self.ga.at[net.col], (net.row, j)))
        elif phase == 4:
            self.out[net.core] = self.ga[...]
            self.flying.append(net.start(self.ga, self.out.at[net.core], other))


class Factor:
    B = 32

    def __init__(self, g, w):
        self.g, self.w, self.block = g, w, 0

    def begin(self):
        r = lax.broadcasted_iota(jnp.int32, (K, K), 0)
        c = lax.broadcasted_iota(jnp.int32, (K, K), 1)
        self.w[...] = (r == c).astype(F32)

    def advance(self):
        b, start = self.B, self.block * self.B
        self.block += 1
        rows = pl.ds(start, b)
        pg, pu = self.g[rows, :], self.w[rows, :]
        sub = lax.broadcasted_iota(jnp.int32, (b, 1), 0)
        for j in range(b):
            col = pg[:, start + j : start + j + 1]
            p = col[j : j + 1, :]
            r = lax.rsqrt(p)
            r = r * (1.5 - 0.5 * p * r * r)
            f = jnp.where(sub > j, col * r, 0.0)
            sg, su = pg[j : j + 1, :] * r, pu[j : j + 1, :] * r
            pg = jnp.where(sub == j, sg, pg - f * sg)
            pu = jnp.where(sub == j, su, pu - f * su)
        self.w[rows, :] = pu
        if start + b < K:
            lane = lax.broadcasted_iota(jnp.int32, (b, K), 1)
            low = jnp.where(lane >= start + b, pg, 0.0)
            down = (((0,), (0,)), ((), ()))
            self.g[...] = self.g[...] - lax.dot_general(low, low, down, precision=HI, preferred_element_type=F32)
            self.w[...] = self.w[...] - lax.dot_general(low, pu, down, precision=HI, preferred_element_type=F32)


def gram(v):
    return lax.dot_general(v, v, (((0,), (0,)), ((), ())), precision=HI, preferred_element_type=F32)


def times_t(v, w):
    return lax.dot_general(v, w, (((1,), (1,)), ((), ())), precision=HI, preferred_element_type=F32)


def main_kernel(
    slot_ref, tiles_hbm, sketch_hbm,
    f_out, w_out, s_out, g_out,
    tiles, dense, sketch, part, ra0, ra1, ra2, ra3, rb0, rb1, rb2, rb3,
    blocks, xt, bp, sb, rc, sz0, sz1, rz0, rz1, bt,
    gm, gh, gr0, gr1, gr2, ga, gfull, gwork, winv,
    load_sem, send_sem, recv_sem,
):
    net = Net(send_sem, recv_sem)
    load_tiles = pltpu.make_async_copy(tiles_hbm, tiles.at[pl.ds(0, tiles_hbm.shape[0])], load_sem.at[0])
    load_sketch = pltpu.make_async_copy(sketch_hbm, sketch, load_sem.at[1])
    load_tiles.start()
    load_sketch.start()

    barrier = pltpu.get_barrier_semaphore()
    for n in range(1, 16):
        pl.semaphore_signal(barrier, inc=1, device_id=(net.row, (net.col + n) % 16), device_id_type=MESH)
    for n in range(1, 4):
        pl.semaphore_signal(barrier, inc=1, device_id=net.to(z=(net.z + n) % 4), device_id_type=MESH)
    pl.semaphore_signal(barrier, inc=1, device_id=net.to(core=1 - net.core), device_id_type=MESH)

    tiles[tiles_hbm.shape[0]] = jnp.zeros((TILE, TILE), BF16)
    load_tiles.wait()

    def place(i, _):
        for j in range(CB):
            dense[pl.ds(pl.multiple_of(i * TILE, TILE), TILE), pl.ds(j * TILE, TILE)] = tiles[slot_ref[i * CB + j]]
        return 0

    lax.fori_loop(0, RB, place, 0)
    load_sketch.wait()
    pl.semaphore_wait(barrier, 19)

    step = 512

    def product_one(n, _):
        m, k = n // 8, n % 8
        a = dense[pl.ds(pl.multiple_of(m * step, step), step), pl.ds(pl.multiple_of(k * step, step), step)]
        b = sketch[pl.ds(pl.multiple_of(k * step, step), step), :]
        value = jnp.dot(a, b, preferred_element_type=F32).reshape(4, 4, 32, K)
        part[m] = jnp.where(k == 0, value, part[m] + value)
        return 0

    lax.fori_loop(0, 32, product_one, 0)
    reduce_scatter(net, part, ra0, ra1, ra2, ra3)

    first = part[net.x, net.y].reshape(TILE, K)
    f_out[...] = first
    first_t = first.T
    high = first_t.astype(BF16)
    low = (first_t - high.astype(F32)).astype(BF16)
    for q in range(4):
        blocks[net.x, net.y, q, 0] = high[q * 64 : q * 64 + 64, :]
        blocks[net.x, net.y, q, 1] = low[q * 64 : q * 64 + 64, :]
    gather = Gather(net, blocks)
    gather.advance()
    gm[0] = gram(first)
    sums = [
        GramSum(net, gm.at[i], gh.at[i], gr0.at[i], gr1.at[i], gr2.at[i], ga.at[i], gfull.at[i]) for i in range(2)
    ]
    sums[0].advance()
    gather.advance()
    sums[0].advance()
    gather.advance()
    gather.advance()
    sums[0].advance()
    gather.advance()
    sums[0].advance()

    for n in range(16):
        xt[:, n * TILE : (n + 1) * TILE] = blocks[n // 4, n % 4].reshape(2 * K, TILE)

    def product_two(core):
        def body(n, _):
            p = n // 2 * 2 + core
            col = pl.multiple_of(p * 512 + n % 2 * 256, 256)
            value = jnp.dot(xt[...], dense[:, pl.ds(col, 256)], preferred_element_type=F32)
            value = jnp.sum(value.reshape(4, 2, 64, 256), axis=1).reshape(K, 256)
            bp[p, :, pl.ds(pl.multiple_of(n % 2 * 256, 256), 256)] = value
            return 0

        lax.fori_loop(0, 8, body, 0)

    other = net.to(core=1 - net.core)
    product_two(1 - net.core)
    copies = []
    for z in range(4):
        sb[z] = bp[2 * z + 1 - net.core].astype(BF16)
        copies.append(net.start(sb.at[z], rc.at[z], other))
    product_two(net.core)
    sums[0].advance()
    for z in range(4):
        copies[z].wait_recv()
        p = 2 * z + net.core
        bp[p] = bp[p] + rc[z].astype(F32)

    sums[0].advance()
    factor = Factor(gwork, winv)
    gwork[...] = gfull[0].reshape(K, K)
    factor.begin()

    half = K // 2
    edges = ((1, 3), (3, 1))
    zc = []
    for h, (e, g) in enumerate(edges):
        rows = pl.ds(h * half, half)
        to = net.to(z=flip(net.z, e))
        for i, k in enumerate((e, 2)):
            sz0[h, i] = bp[2 * flip(net.z, k) + net.core, rows, :].astype(BF16)
            zc.append(net.start(sz0.at[h, i], rz0.at[h, i], to))
    factor.advance()
    factor.advance()
    zd = []
    for h, (e, g) in enumerate(edges):
        rows = pl.ds(h * half, half)
        zc[2 * h + 1].wait_recv()
        p = 2 * flip(net.z, g) + net.core
        sz1[h] = (bp[p, rows, :] + rz0[h, 1].astype(F32)).astype(BF16)
        zd.append(net.start(sz1.at[h], rz1.at[h], net.to(z=flip(net.z, g))))
    factor.advance()
    ze = []
    for h, (e, g) in enumerate(edges):
        rows = pl.ds(h * half, half)
        zc[2 * h].wait_recv()
        zd[h].wait_recv()
        p = 2 * net.z + net.core
        value = bp[p, rows, :] + rz0[h, 0].astype(F32) + rz1[h].astype(F32)
        bt[net.z, net.core, h] = value.astype(BF16)
        ref = bt.at[net.z, net.core, h]
        ze.append(net.start(ref, ref, net.to(z=flip(net.z, e))))
    factor.advance()
    zf = []
    for h, (e, g) in enumerate(edges):
        ze[h].wait_recv()
        for z in (net.z, flip(net.z, e)):
            ref = bt.at[z, net.core, h]
            zf.append(net.start(ref, ref, net.to(z=flip(net.z, g))))
    factor.advance()
    factor.advance()
    for copy in zf:
        copy.wait_recv()
    last = net.start(bt.at[:, net.core], bt.at[:, net.core], other)
    factor.advance()
    factor.advance()
    w_out[...] = winv[...]
    last.wait_recv()

    net.close()

    def product_three(n, _):
        m, k = n // 8, n % 8
        a = dense[pl.ds(pl.multiple_of(m * step, step), step), pl.ds(pl.multiple_of(k * step, step), step)]
        b = bt[k // 2, k % 2].reshape(K, step)
        value = lax.dot_general(a, b, (((1,), (1,)), ((), ())), preferred_element_type=F32).reshape(4, 4, 32, K)
        part[m] = jnp.where(k == 0, value, part[m] + value)
        return 0

    lax.fori_loop(0, 32, product_three, 0)
    reduce_scatter(net, part, rb0, rb1, rb2, rb3)
    second = times_t(part[net.x, net.y].reshape(TILE, K), winv[...])
    s_out[...] = second
    gm[1] = gram(second)
    for _ in range(6):
        sums[1].advance()
    g_out[...] = gfull[1].reshape(K, K)
    net.close()


def last_kernel(scale, f_ref, w_ref, s_ref, g_ref, range_ref, basis_ref, gwork, winv):
    range_ref[...] = times_t(f_ref[...], w_ref[...]) * scale
    gwork[...] = g_ref[...]
    factor = Factor(gwork, winv)
    factor.begin()
    for _ in range(K // Factor.B):
        factor.advance()
    basis_ref[...] = times_t(s_ref[...], winv[...]) * scale


def body(tile_data, tile_rows, tile_cols, tile_count, sketch):
    tiles = tile_data[0, 0]
    total = tiles.shape[0]
    number = jnp.arange(total, dtype=jnp.int32)
    place = tile_rows[0, 0] * CB + tile_cols[0, 0]
    place = jnp.where(number < tile_count[0, 0], place, -1)
    hit = place[None, :] == jnp.arange(RB * CB, dtype=jnp.int32)[:, None]
    slot = jnp.min(jnp.where(hit, number[None, :], total), axis=1)
    vmem = pl.BlockSpec(memory_space=pltpu.VMEM)
    hbm = pl.BlockSpec(memory_space=pl.ANY)
    square = jax.ShapeDtypeStruct((K, K), F32)
    share = jax.ShapeDtypeStruct((TILE, K), F32)

    def stages(dtype):
        return [
            pltpu.VMEM((4, 2, 4, 32, K), dtype),
            pltpu.VMEM((4, 4, 32, K), dtype),
            pltpu.VMEM((4, 2, 32, K), dtype),
            pltpu.VMEM((4, 32, K), dtype),
        ]

    first, inverse, second, gram_two = pl.pallas_call(
        main_kernel,
        out_shape=(share, square, share, square),
        in_specs=[pl.BlockSpec(memory_space=pltpu.SMEM), hbm, hbm],
        out_specs=(vmem,) * 4,
        scratch_shapes=[
            pltpu.VMEM((total + 1, TILE, TILE), BF16),
            pltpu.VMEM((ROWS_DEV, COLS_DEV), BF16),
            pltpu.VMEM((COLS_DEV, K), BF16),
            pltpu.VMEM((4, 4, 4, 32, K), F32),
            *stages(F32),
            *stages(F32),
            pltpu.VMEM((4, 4, 4, 2, 64, TILE), BF16),
            pltpu.VMEM((2 * K, ROWS_DEV), BF16),
            pltpu.VMEM((8, K, 512), F32),
            pltpu.VMEM((4, K, 512), BF16),
            pltpu.VMEM((4, K, 512), BF16),
            pltpu.VMEM((2, 2, K // 2, 512), BF16),
            pltpu.VMEM((2, K // 2, 512), BF16),
            pltpu.VMEM((2, 2, K // 2, 512), BF16),
            pltpu.VMEM((2, K // 2, 512), BF16),
            pltpu.VMEM((4, 2, 2, K // 2, 512), BF16),
            pltpu.VMEM((2, K, K), F32),
            pltpu.VMEM((2, 16, 8, K), F32),
            pltpu.VMEM((2, K // 2, K), F32),
            pltpu.VMEM((2, 16, 8, K), F32),
            pltpu.VMEM((2, 4, 8, K), F32),
            pltpu.VMEM((2, 16, 8, K), F32),
            pltpu.VMEM((2, 2, 16, 8, K), F32),
            pltpu.VMEM((K, K), F32),
            pltpu.VMEM((K, K), F32),
            pltpu.SemaphoreType.DMA((2,)),
            pltpu.SemaphoreType.DMA((COPIES,)),
            pltpu.SemaphoreType.DMA((COPIES,)),
        ],
        compiler_params=pltpu.CompilerParams(
            collective_id=0, has_side_effects=True, vmem_limit_bytes=60 * 1024 * 1024
        ),
        name="range_finder",
    )(slot, tiles, sketch)
    scale = math.sqrt(ROWS_DEV * lax.axis_size("row"))
    return pl.pallas_call(
        lambda *refs: last_kernel(scale, *refs),
        out_shape=(share, share),
        in_specs=[vmem] * 4,
        out_specs=(vmem, vmem),
        scratch_shapes=[pltpu.VMEM((K, K), F32)] * 2,
        name="finish",
    )(first, inverse, second, gram_two)


def solution(mesh):
    placed = (
        P("row", "col", None, None, None),
        P("row", "col", None),
        P("row", "col", None),
        P("row", "col"),
        P("col", None),
    )
    return jax.shard_map(
        body,
        mesh=mesh,
        in_specs=placed,
        out_specs=(P(("row", "col"), None), P(("row", "col"), None)),
        check_vma=False,
    )
```

```python
import math

import jax
import jax.numpy as jnp
from jax import lax
from jax.experimental import pallas as pl
from jax.experimental.pallas import tpu as pltpu
from jax.sharding import PartitionSpec as P

MESH = pl.DeviceIdType.MESH
F32, BF16 = jnp.float32, jnp.bfloat16
HI = lax.Precision.HIGHEST
TILE, K, RB, CB = 128, 256, 16, 32
ROWS_DEV, COLS_DEV = RB * TILE, CB * TILE
COPIES = 208


def flip(c, e):
    return (c // 2 + e // 2) % 2 * 2 + (c + e) % 2


ORDERS = ((0, 1, 3), (0, 3, 1), (1, 1, 3), (1, 3, 1))
ALL = slice(None)


class Copy:
    def __init__(self, net, number, make):
        self.net, self.number, self.make = net, number, make

    def copy(self):
        src, dst, device = self.make()
        return pltpu.make_async_remote_copy(
            src_ref=src, dst_ref=dst, send_sem=self.net.send.at[self.number], recv_sem=self.net.recv.at[self.number],
            device_id=device, device_id_type=MESH,
        )

    def start(self):
        self.copy().start()
        return self

    def wait(self):
        self.copy().wait_recv()


class Net:
    def __init__(self, send, recv):
        self.send, self.recv, self.count = send, recv, 0
        self.open = []
        r, c = lax.axis_index("row"), lax.axis_index("col")
        self.z, self.core, self.x, self.y = r // 2, r % 2, c // 4, c % 4
        self.row, self.col = r, c
        self.pos = (self.x, self.y)

    def to(self, x=None, y=None, z=None, core=None):
        x = self.x if x is None else x
        y = self.y if y is None else y
        z = self.z if z is None else z
        core = self.core if core is None else core
        return (z * 2 + core, x * 4 + y)

    def peer(self, axis, e):
        return self.to(x=flip(self.x, e)) if axis == 0 else self.to(y=flip(self.y, e))

    def plan(self, make):
        copy = Copy(self, self.count, make)
        self.count += 1
        self.open.append(copy)
        return copy

    def family(self, n, make):
        base = self.count
        self.count += n
        self.open += [Copy(self, base + t, lambda t=t: make(t)) for t in range(n)]
        return lambda t: Copy(self, base + t, lambda: make(t))

    def start(self, make):
        return self.plan(make).start()

    def close(self):
        for copy in self.open:
            copy.copy().wait_send()
        self.open = []


def at2(ref, axis, a, b, *rest):
    return ref.at[(a, b, *rest)] if axis == 0 else ref.at[(b, a, *rest)]


def reduce_scatter(net, part, r0, r1, r2, r3, compute):
    def add(axis, a, b, q, value):
        ref = at2(part, axis, a, b, q)
        ref[...] = ref[...] + value

    first, across = {}, {}
    for q in (0, 1):
        _, e, g = ORDERS[q]
        for i, k in enumerate((e, 2)):
            first[q, i] = net.plan(
                lambda q=q, i=i, k=k, e=e: (part.at[flip(net.x, k), :, q], r0.at[q, i], net.peer(0, e))
            )
    for q in (2, 3):
        _, e, g = ORDERS[q]
        for i, k in enumerate((e, 2)):
            across[q, i] = net.family(
                4,
                lambda t, q=q, i=i, k=k, e=e: (
                    part.at[flip(net.x, (t + 1) % 4), flip(net.y, k), q],
                    r0.at[q, i, flip(net.x, (t + 1) % 4)],
                    net.peer(1, e),
                ),
            )

    def step(t, _):
        compute(flip(net.x, (t + 1) % 4))
        for key in across:
            across[key](t).start()
        for now, keys in ((0, [(0, 0)]), (1, [(0, 1), (1, 1)]), (2, [(1, 0)])):

            @pl.when(t == now)
            def _():
                for key in keys:
                    first[key].start()

        return 0

    lax.fori_loop(0, 4, step, 0)

    def wait_first(q, i):
        if q < 2:
            first[q, i].wait()
        else:
            for t in range(4):
                across[q, i](t).wait()

    second, third, fourth = {}, {}, {}
    for q, (axis, e, g) in enumerate(ORDERS):
        c = net.pos[axis]
        wait_first(q, 1)
        add(axis, flip(c, g), ALL, q, r0[q, 1])
        second[q] = net.start(
            lambda q=q, axis=axis, g=g: (at2(part, axis, flip(net.pos[axis], g), ALL, q), r1.at[q], net.peer(axis, g))
        )
        wait_first(q, 0)
        add(axis, c, ALL, q, r0[q, 0])
    for q, (axis, e, g) in enumerate(ORDERS):
        c, other = net.pos[axis], 1 - axis
        second[q].wait()
        add(axis, c, ALL, q, r1[q])
        for i, k in enumerate((e, 2)):
            third[q, i] = net.start(
                lambda q=q, i=i, k=k, axis=axis, other=other, e=e: (
                    at2(part, other, flip(net.pos[other], k), net.pos[axis], q), r2.at[q, i], net.peer(other, e)
                )
            )
    for q, (axis, e, g) in enumerate(ORDERS):
        c, d, other = net.pos[axis], net.pos[1 - axis], 1 - axis
        third[q, 1].wait()
        add(axis, c, flip(d, g), q, r2[q, 1])
        fourth[q] = net.start(
            lambda q=q, axis=axis, other=other, g=g: (
                at2(part, other, flip(net.pos[other], g), net.pos[axis], q), r3.at[q], net.peer(other, g)
            )
        )
        third[q, 0].wait()
        add(axis, c, d, q, r2[q, 0])
    for q, (axis, e, g) in enumerate(ORDERS):
        fourth[q].wait()
        add(axis, net.pos[axis], net.pos[1 - axis], q, r3[q])


class Gather:
    def __init__(self, net, buf):
        self.net, self.buf, self.step, self.flying = net, buf, 0, []

    def advance(self):
        net, buf, t = self.net, self.buf, self.step
        for copy in self.flying:
            copy.wait()
        self.flying = []
        self.step += 1
        if t == 4:
            return
        for q, (axis, e, g) in enumerate(ORDERS):
            other = 1 - axis
            link = ((axis, e), (axis, g), (other, e), (other, g))[t]
            moves = ((0, 0),) if t == 0 else ((0, 0), (e, 0)) if t == 1 else ((None, 0),) if t == 2 else ((None, 0), (None, e))
            for i, j in moves:

                def make(q=q, axis=axis, link=link, i=i, j=j):
                    a = ALL if i is None else flip(net.pos[axis], i)
                    ref = at2(buf, axis, a, flip(net.pos[1 - axis], j), q)
                    return ref, ref, net.peer(*link)

                self.flying.append(net.start(make))


class GramSum:
    def __init__(self, net, g, h, r0, r1, r2, ga, out):
        self.net, self.g, self.h, self.r0, self.r1, self.r2, self.ga, self.out = net, g, h, r0, r1, r2, ga, out
        self.phase, self.flying = 0, []

    def advance(self):
        net, half = self.net, K // 2
        for copy in self.flying:
            copy.wait()
        self.flying = []
        phase = self.phase
        self.phase += 1

        def rows(core):
            return pl.ds(pl.multiple_of(core * half, half), half)

        def send(make):
            self.flying.append(net.start(make))

        if phase == 0:
            send(lambda: (self.g.at[rows(1 - net.core)], self.r0, net.to(core=1 - net.core)))
        elif phase == 1:
            self.h[...] = (self.g[rows(net.core), :] + self.r0[...]).reshape(16, 8, K)
            for n in range(1, 16):
                send(lambda n=n: (self.h.at[(net.col + n) % 16], self.r1.at[n], (net.row, (net.col + n) % 16)))
            self.r1[0] = self.h[net.col]
        elif phase == 2:
            self.r2[net.z] = jnp.sum(self.r1[...], axis=0)
            for n in range(1, 4):
                send(lambda n=n: (self.r2.at[net.z], self.r2.at[net.z], net.to(z=(net.z + n) % 4)))
        elif phase == 3:
            self.ga[net.col] = jnp.sum(self.r2[...], axis=0)
            for n in range(1, 16):
                send(lambda n=n: (self.ga.at[net.col], self.ga.at[net.col], (net.row, (net.col + n) % 16)))
        elif phase == 4:
            self.out[net.core] = self.ga[...]
            send(lambda: (self.ga, self.out.at[net.core], net.to(core=1 - net.core)))


class Factor:
    B, S = 64, 8

    def __init__(self, g, w):
        self.g, self.w, self.block = g, w, 0

    def begin(self):
        r = lax.broadcasted_iota(jnp.int32, (K, K), 0)
        c = lax.broadcasted_iota(jnp.int32, (K, K), 1)
        self.w[...] = (r == c).astype(F32)

    def advance(self):
        b, start = self.B, self.block * self.B
        self.block += 1
        rows = pl.ds(start, b)
        pg, pu = self.g[rows, :], self.w[rows, :]
        sub = lax.broadcasted_iota(jnp.int32, (b, 1), 0)
        wide = lax.broadcasted_iota(jnp.int32, (b, 128), 0)
        for s in range(0, b, self.S):
            at = start + s
            cols = [jnp.broadcast_to(pg[:, at + k : at + k + 1], (b, 128)) for k in range(self.S)]
            factors, roots = [], []
            for k in range(self.S):
                p = cols[k][s + k : s + k + 1, :]
                r = lax.rsqrt(p)
                r = r * (1.5 - 0.5 * p * r * r)
                f = cols[k] * r
                for m in range(k + 1, self.S):
                    cols[m] = cols[m] - f * f[s + m : s + m + 1, :]
                factors.append(jnp.where(wide > s + k, f, 0.0))
                roots.append(r)
            for k in range(self.S):
                r = jnp.concatenate([roots[k], roots[k]], axis=1)
                f = jnp.concatenate([factors[k], factors[k]], axis=1)
                sg, su = pg[s + k : s + k + 1, :] * r, pu[s + k : s + k + 1, :] * r
                pg = jnp.where(sub == s + k, sg, pg - f * sg)
                pu = jnp.where(sub == s + k, su, pu - f * su)
        self.w[rows, :] = pu
        if start + b < K:
            lane = lax.broadcasted_iota(jnp.int32, (b, K), 1)
            low = jnp.where(lane >= start + b, pg, 0.0)
            down = (((0,), (0,)), ((), ()))
            self.g[...] = self.g[...] - lax.dot_general(low, low, down, precision=HI, preferred_element_type=F32)
            self.w[...] = self.w[...] - lax.dot_general(low, pu, down, precision=HI, preferred_element_type=F32)


def gram(v):
    return lax.dot_general(v, v, (((0,), (0,)), ((), ())), precision=HI, preferred_element_type=F32)


def times_t(v, w):
    return lax.dot_general(v, w, (((1,), (1,)), ((), ())), precision=HI, preferred_element_type=F32)


def main_kernel(
    slot_ref, tiles_hbm, sketch_hbm,
    f_out, w_out, s_out, g_out,
    tiles, dense, sketch, part, ra0, ra1, ra2, ra3, rb0, rb1, rb2, rb3,
    blocks, xt, bp, sb, rc, sz0, sz1, rz0, rz1, bt,
    gm, gh, gr0, gr1, gr2, ga, gfull, gwork, winv,
    load_sem, send_sem, recv_sem,
):
    net = Net(send_sem, recv_sem)
    load_tiles = pltpu.make_async_copy(tiles_hbm, tiles.at[pl.ds(0, tiles_hbm.shape[0])], load_sem.at[0])
    load_sketch = pltpu.make_async_copy(sketch_hbm, sketch, load_sem.at[1])
    load_tiles.start()
    load_sketch.start()

    barrier = pltpu.get_barrier_semaphore()
    for n in range(1, 16):
        pl.semaphore_signal(barrier, inc=1, device_id=(net.row, (net.col + n) % 16), device_id_type=MESH)
    for n in range(1, 4):
        pl.semaphore_signal(barrier, inc=1, device_id=net.to(z=(net.z + n) % 4), device_id_type=MESH)
    pl.semaphore_signal(barrier, inc=1, device_id=net.to(core=1 - net.core), device_id_type=MESH)

    tiles[tiles_hbm.shape[0]] = jnp.zeros((TILE, TILE), BF16)
    load_tiles.wait()

    def place(i, _):
        for j in range(CB):
            dense[pl.ds(pl.multiple_of(i * TILE, TILE), TILE), pl.ds(j * TILE, TILE)] = tiles[slot_ref[i * CB + j]]
        return 0

    lax.fori_loop(0, RB, place, 0)
    load_sketch.wait()
    pl.semaphore_wait(barrier, 19)

    step = 512

    def rows_of(m):
        return pl.ds(pl.multiple_of(m * step, step), step)

    def product_one(m):
        part[m] = jnp.dot(dense[rows_of(m), :], sketch[...], preferred_element_type=F32).reshape(4, 4, 32, K)

    reduce_scatter(net, part, ra0, ra1, ra2, ra3, product_one)

    first = part[net.x, net.y].reshape(TILE, K)
    f_out[...] = first
    first_t = first.T
    high = first_t.astype(BF16)
    low = (first_t - high.astype(F32)).astype(BF16)
    for q in range(4):
        blocks[net.x, net.y, q, 0] = high[q * 64 : q * 64 + 64, :]
        blocks[net.x, net.y, q, 1] = low[q * 64 : q * 64 + 64, :]
    gather = Gather(net, blocks)
    sums = [
        GramSum(net, gm.at[i], gh.at[i], gr0.at[i], gr1.at[i], gr2.at[i], ga.at[i], gfull.at[i]) for i in range(2)
    ]
    gather.advance()
    gm[0] = gram(first)
    sums[0].advance()
    gather.advance()
    gather.advance()
    sums[0].advance()
    gather.advance()
    gather.advance()

    for n in range(16):
        xt[:, n * TILE : (n + 1) * TILE] = blocks[n // 4, n % 4].reshape(2 * K, TILE)

    half = K // 2
    edges = ((1, 3), (3, 1))

    def piece(z, core):
        return pl.ds(pl.multiple_of((2 * z + core) * step, step), step)

    def product_two(z, core):
        value = jnp.dot(xt[...], dense[:, piece(z, core)], preferred_element_type=F32)
        return jnp.sum(value.reshape(4, 2, 64, step), axis=1).reshape(K, step)

    def z_of(t):
        return flip(net.z, (t + 1) % 4)

    swap = net.family(4, lambda t: (sb.at[z_of(t)], rc.at[z_of(t)], net.to(core=1 - net.core)))
    zc = {
        (h, i): net.plan(lambda h=h, i=i, e=e: (sz0.at[h, i], rz0.at[h, i], net.to(z=flip(net.z, e))))
        for h, (e, g) in enumerate(edges)
        for i in range(2)
    }

    def cross_step(t, _):
        z = z_of(t)
        sb[z] = product_two(z, 1 - net.core).astype(BF16)
        swap(t).start()
        bp[z] = product_two(z, net.core)
        swap(t).wait()
        bp[z] = bp[z] + rc[z].astype(F32)
        for now, keys in ((0, [(0, 0)]), (1, [(0, 1), (1, 1)]), (2, [(1, 0)])):

            @pl.when(t == now)
            def _():
                for h, i in keys:
                    sz0[h, i] = bp[z, h * half : (h + 1) * half, :].astype(BF16)
                    zc[h, i].start()

        return 0

    lax.fori_loop(0, 2, cross_step, 0)
    sums[0].advance()
    lax.fori_loop(2, 4, cross_step, 0)
    sums[0].advance()

    zd = []
    for h, (e, g) in enumerate(edges):
        zc[h, 1].wait()
        sz1[h] = (bp[flip(net.z, g), h * half : (h + 1) * half, :] + rz0[h, 1].astype(F32)).astype(BF16)
        zd.append(net.start(lambda h=h, g=g: (sz1.at[h], rz1.at[h], net.to(z=flip(net.z, g)))))
    sums[0].advance()

    def bt_at(z, core, h):
        return bt.at[pl.ds(h * half, half), piece(z, core)]

    ze = []
    for h, (e, g) in enumerate(edges):
        zc[h, 0].wait()
        zd[h].wait()
        value = bp[net.z, h * half : (h + 1) * half, :] + rz0[h, 0].astype(F32) + rz1[h].astype(F32)
        bt[pl.ds(h * half, half), piece(net.z, net.core)] = value.astype(BF16)

        def make(h=h, e=e):
            ref = bt_at(net.z, net.core, h)
            return ref, ref, net.to(z=flip(net.z, e))

        ze.append(net.start(make))
    sums[0].advance()
    factor = Factor(gwork, winv)
    gwork[...] = gfull[0].reshape(K, K)
    factor.begin()
    factor.advance()
    zf = []
    for h, (e, g) in enumerate(edges):
        ze[h].wait()
        for k in (0, e):

            def make(h=h, g=g, k=k):
                ref = bt_at(flip(net.z, k), net.core, h)
                return ref, ref, net.to(z=flip(net.z, g))

            zf.append(net.start(make))
    factor.advance()
    factor.advance()
    for copy in zf:
        copy.wait()
    last = []
    for z in range(4):

        def make(z=z):
            ref = bt.at[:, piece(z, net.core)]
            return ref, ref, net.to(core=1 - net.core)

        last.append(net.start(make))
    factor.advance()
    w_out[...] = winv[...]
    for copy in last:
        copy.wait()

    net.close()

    def product_three(m):
        value = lax.dot_general(dense[rows_of(m), :], bt[...], (((1,), (1,)), ((), ())), preferred_element_type=F32)
        part[m] = value.reshape(4, 4, 32, K)

    reduce_scatter(net, part, rb0, rb1, rb2, rb3, product_three)
    second = times_t(part[net.x, net.y].reshape(TILE, K), winv[...])
    s_out[...] = second
    gm[1] = gram(second)
    for _ in range(6):
        sums[1].advance()
    g_out[...] = gfull[1].reshape(K, K)
    net.close()


def last_kernel(scale, f_ref, w_ref, s_ref, g_ref, range_ref, basis_ref, gwork, winv):
    range_ref[...] = times_t(f_ref[...], w_ref[...]) * scale
    gwork[...] = g_ref[...]
    factor = Factor(gwork, winv)
    factor.begin()
    for _ in range(K // Factor.B):
        factor.advance()
    basis_ref[...] = times_t(s_ref[...], winv[...]) * scale


def body(tile_data, tile_rows, tile_cols, tile_count, sketch):
    tiles = tile_data[0, 0]
    total = tiles.shape[0]
    number = jnp.arange(total, dtype=jnp.int32)
    place = tile_rows[0, 0] * CB + tile_cols[0, 0]
    place = jnp.where(number < tile_count[0, 0], place, -1)
    hit = place[None, :] == jnp.arange(RB * CB, dtype=jnp.int32)[:, None]
    slot = jnp.min(jnp.where(hit, number[None, :], total), axis=1)
    vmem = pl.BlockSpec(memory_space=pltpu.VMEM)
    hbm = pl.BlockSpec(memory_space=pl.ANY)
    square = jax.ShapeDtypeStruct((K, K), F32)
    share = jax.ShapeDtypeStruct((TILE, K), F32)

    def stages(dtype):
        return [
            pltpu.VMEM((4, 2, 4, 32, K), dtype),
            pltpu.VMEM((4, 4, 32, K), dtype),
            pltpu.VMEM((4, 2, 32, K), dtype),
            pltpu.VMEM((4, 32, K), dtype),
        ]

    first, inverse, second, gram_two = pl.pallas_call(
        main_kernel,
        out_shape=(share, square, share, square),
        in_specs=[pl.BlockSpec(memory_space=pltpu.SMEM), hbm, hbm],
        out_specs=(vmem,) * 4,
        scratch_shapes=[
            pltpu.VMEM((total + 1, TILE, TILE), BF16),
            pltpu.VMEM((ROWS_DEV, COLS_DEV), BF16),
            pltpu.VMEM((COLS_DEV, K), BF16),
            pltpu.VMEM((4, 4, 4, 32, K), F32),
            *stages(F32),
            *stages(F32),
            pltpu.VMEM((4, 4, 4, 2, 64, TILE), BF16),
            pltpu.VMEM((2 * K, ROWS_DEV), BF16),
            pltpu.VMEM((4, K, 512), F32),
            pltpu.VMEM((4, K, 512), BF16),
            pltpu.VMEM((4, K, 512), BF16),
            pltpu.VMEM((2, 2, K // 2, 512), BF16),
            pltpu.VMEM((2, K // 2, 512), BF16),
            pltpu.VMEM((2, 2, K // 2, 512), BF16),
            pltpu.VMEM((2, K // 2, 512), BF16),
            pltpu.VMEM((K, COLS_DEV), BF16),
            pltpu.VMEM((2, K, K), F32),
            pltpu.VMEM((2, 16, 8, K), F32),
            pltpu.VMEM((2, K // 2, K), F32),
            pltpu.VMEM((2, 16, 8, K), F32),
            pltpu.VMEM((2, 4, 8, K), F32),
            pltpu.VMEM((2, 16, 8, K), F32),
            pltpu.VMEM((2, 2, 16, 8, K), F32),
            pltpu.VMEM((K, K), F32),
            pltpu.VMEM((K, K), F32),
            pltpu.SemaphoreType.DMA((2,)),
            pltpu.SemaphoreType.DMA((COPIES,)),
            pltpu.SemaphoreType.DMA((COPIES,)),
        ],
        compiler_params=pltpu.CompilerParams(
            collective_id=0, has_side_effects=True, vmem_limit_bytes=60 * 1024 * 1024
        ),
        name="range_finder",
    )(slot, tiles, sketch)
    scale = math.sqrt(ROWS_DEV * lax.axis_size("row"))
    return pl.pallas_call(
        lambda *refs: last_kernel(scale, *refs),
        out_shape=(share, share),
        in_specs=[vmem] * 4,
        out_specs=(vmem, vmem),
        scratch_shapes=[pltpu.VMEM((K, K), F32)] * 2,
        name="finish",
    )(first, inverse, second, gram_two)


def solution(mesh):
    placed = (
        P("row", "col", None, None, None),
        P("row", "col", None),
        P("row", "col", None),
        P("row", "col"),
        P("col", None),
    )
    return jax.shard_map(
        body,
        mesh=mesh,
        in_specs=placed,
        out_specs=(P(("row", "col"), None), P(("row", "col"), None)),
        check_vma=False,
    )
```
